512 devices in a mesh: dp: 8 (over z_lo), seq: 64 (over x, z_hi, y, core).
Axes of the slice: x: 4, y: 4, z: 16 (z_hi: 2, z_lo: 8; z = z_hi * 8 + z_lo), core: 2. Of those that a mesh axis runs over, the one named last changes fastest.
Arguments:
- queries: bfloat16 [8, 8192, 2048], P('dp', 'seq'), may hold values from -60 to 60
- raw_key_rows: bfloat16 [8, 8192, 1024], P('dp', 'seq'), may hold values from -60 to 60
- values: bfloat16 [8, 8192, 1024], P('dp', 'seq'), may hold values from -6 to 6
- out_grad: bfloat16 [8, 8192, 2048], P('dp', 'seq'), may hold values from -96 to 96
- query_gain: float32 [128], P('dp'), may hold values from 0.5 to 6
- key_norm_gain: float32 [128], P('dp'), may hold values from 0.5 to 6
Outputs:
- query_grad: bfloat16 [8, 8192, 2048], P('dp', 'seq')
- key_gradient: bfloat16 [8, 8192, 1024], P('dp', 'seq')
- value_gradient: bfloat16 [8, 8192, 1024], P('dp', 'seq')
The draws below stay inside these ranges and needn't reach their ends.
All inputs are finite; a program needn't handle non-finite values.
Results may differ from the reference program's by a relative error of at most 0.04.
The reference program's roundings to bfloat16 on the way count: a program that leaves them out, or rounds other values in their place, can miss the bound.
Values may be sent and summed in bfloat16 or wider, within the bound.
A program may use at most 64 MiB of HBM per device.

```python
import math
import jax
import jax.numpy as jnp
from jax import lax

TOK_DEV = 128
QUERY_HEADS = 16
KEY_VALUE_HEADS = 8
HEAD_SIZE = 128
WINDOW_KEYS = 1024
SEQUENCE_COUNT = 8
TOKEN_COUNT = 8192
N_SEQ = 64


def coarse_field(key, heads):
    shape = (SEQUENCE_COUNT, TOKEN_COUNT, heads, HEAD_SIZE)
    rotary_base = jnp.clip(jax.random.normal(jax.random.fold_in(key, 1), shape, jnp.float32), -4.0, 4.0)
    row_scale = jnp.exp(jax.random.uniform(jax.random.fold_in(key, 2), (SEQUENCE_COUNT, TOKEN_COUNT, heads, 1), jnp.float32, math.log(1.0 / 3.0), math.log(3.0)))
    channel_scale = jnp.exp(jax.random.uniform(jax.random.fold_in(key, 3), (1, 1, heads, HEAD_SIZE), jnp.float32, math.log(0.3), math.log(3.0)))
    return rotary_base * row_scale * channel_scale


def draw_queries(key, part):
    gradient_field = coarse_field(jax.random.fold_in(key, 21), QUERY_HEADS)
    return jnp.clip(gradient_field, -60.0, 60.0).reshape(SEQUENCE_COUNT, TOKEN_COUNT, QUERY_HEADS * HEAD_SIZE).astype(jnp.bfloat16)


def draw_raw_key_rows(key, part):
    gradient_field = coarse_field(jax.random.fold_in(key, 22), KEY_VALUE_HEADS)
    return jnp.clip(gradient_field, -60.0, 60.0).reshape(SEQUENCE_COUNT, TOKEN_COUNT, KEY_VALUE_HEADS * HEAD_SIZE).astype(jnp.bfloat16)


def draw_gain_common(key):
    return jnp.exp(jax.random.uniform(key, (HEAD_SIZE,), jnp.float32, math.log(0.5), math.log(2.0)))


def draw_query_gain(key, part):
    return draw_gain_common(jax.random.fold_in(key, 31))


def draw_key_norm_gain(key, part):
    return draw_gain_common(jax.random.fold_in(key, 32))


def steps_of(key, dims, shards, low, largest):
    def one(dim, parts):
        draws = jax.random.uniform(jax.random.fold_in(jax.random.fold_in(key, 6), dim), (parts,), jnp.float32, low / len(shards), largest / len(shards))
        return jnp.repeat(jnp.exp(draws), dims[dim] // parts).reshape((-1,) + (1,) * (len(dims) - dim - 1))

    level = one(*shards[0])
    for cut in shards[1:]:
        level = level * one(*cut)
    return level


def noise(rng, extent, scale, bound, cuts=(), kind=jnp.bfloat16):
    drawn = scale * jax.random.normal(rng, extent, jnp.float32)
    if cuts:
        drawn = drawn * steps_of(rng, extent, cuts, -0.22, 0.18)
    return jnp.clip(drawn, -bound, bound).astype(kind)


def setup_inputs(seed: int = 0) -> dict:
    seeds = jax.random.split(jax.random.key(seed), 7)
    return {
        "queries": draw_queries(jax.random.fold_in(seeds[6], 71), 0),
        "raw_key_rows": draw_raw_key_rows(jax.random.fold_in(seeds[6], 71), 0),
        "values": noise(seeds[2], (SEQUENCE_COUNT, TOKEN_COUNT, KEY_VALUE_HEADS * HEAD_SIZE), 1.0, 6.0, ((0, 8), (1, 64))),
        "out_grad": noise(seeds[3], (SEQUENCE_COUNT, TOKEN_COUNT, QUERY_HEADS * HEAD_SIZE), 16.0, 96.0, ((0, 8), (1, 64))),
        "query_gain": draw_query_gain(jax.random.fold_in(seeds[6], 71), 0),
        "key_norm_gain": draw_key_norm_gain(jax.random.fold_in(seeds[6], 71), 0),
    }


SCALE = 168.0 ** (-0.5)
ROPE_BASE = 10000.0
EPSILON = 1e-06

def prepare_inputs(input_arrays, gain, token_positions):
    depth = input_arrays.shape[-1]
    half_depth = depth // 2
    inverse = lax.rsqrt(lax.optimization_barrier(jnp.mean(input_arrays * input_arrays, axis=-1, keepdims=True)) + EPSILON)
    normed = input_arrays * inverse * gain
    frequency = ROPE_BASE ** (-jnp.arange(half_depth).astype(input_arrays.dtype) * (2.0 / depth))
    angles = token_positions.astype(input_arrays.dtype)[:, None] * frequency[None, :]
    cosine = jnp.cos(angles)[:, None, :]
    sine_val = jnp.sin(angles)[:, None, :]
    first_half = normed[..., :half_depth]
    second_half = normed[..., half_depth:]
    return jnp.concatenate([first_half * cosine - second_half * sine_val, second_half * cosine + first_half * sine_val], axis=-1)

def visible(anchor, row_list, span):
    query_pos = anchor + jnp.arange(row_list, dtype=jnp.int32)
    key_pos = anchor - WINDOW_KEYS + jnp.arange(span, dtype=jnp.int32)
    return (key_pos[None, :] >= 0) & (key_pos[None, :] > query_pos[:, None] - WINDOW_KEYS) & (key_pos[None, :] <= query_pos[:, None])

def attend_head(operands, mask_table):
    query_group, key_block, value_block, grad_group = operands
    query_wide = query_group.astype(jnp.float32)
    key_wide = key_block.astype(jnp.float32)
    value_wide = value_block.astype(jnp.float32)
    grad_wide = grad_group.astype(jnp.float32)
    scores = SCALE * jnp.einsum('gtd,ld->gtl', query_wide, key_wide)
    scores = jnp.where(mask_table[None], scores, -1e+30)
    row_max = lax.optimization_barrier(jnp.max(scores, axis=-1, keepdims=True))
    weights = jnp.exp(scores - row_max)
    probs = weights / lax.optimization_barrier(jnp.sum(weights, axis=-1, keepdims=True))
    probs_b = probs.astype(jnp.bfloat16)
    attn_out = jnp.einsum('gtl,ld->gtd', probs_b.astype(jnp.float32), value_wide)
    dprob = jnp.einsum('gtd,ld->gtl', grad_wide, value_wide)
    delta = lax.optimization_barrier(jnp.sum(grad_wide * attn_out, axis=-1, keepdims=True))
    dscore_b = (probs * (dprob - delta)).astype(jnp.bfloat16)
    dscore_wide = dscore_b.astype(jnp.float32)
    dq_part = SCALE * jnp.einsum('gtl,ld->gtd', dscore_wide, key_wide)
    dk_part = SCALE * jnp.einsum('gtl,gtd->ld', dscore_wide, query_wide)
    dv_part = jnp.einsum('gtl,gtd->ld', probs_b.astype(jnp.float32), grad_wide)
    return (dq_part, dk_part, dv_part)

def head_terms(query_tile, key_block, value_block, gradient_block, mask_table):
    row_list = query_tile.shape[0]
    group_width = QUERY_HEADS // KEY_VALUE_HEADS
    query_group_rows = query_tile.reshape(row_list, KEY_VALUE_HEADS, group_width, HEAD_SIZE).transpose(1, 2, 0, 3)
    gradient_groups = gradient_block.reshape(row_list, KEY_VALUE_HEADS, group_width, HEAD_SIZE).transpose(1, 2, 0, 3)
    key_heads = key_block.transpose(1, 0, 2)
    value_head_rows = value_block.transpose(1, 0, 2)
    dq_part, dk_part, dv_part = lax.map(lambda operands: attend_head(operands, mask_table), (query_group_rows, key_heads, value_head_rows, gradient_groups))
    return (dq_part.transpose(2, 0, 1, 3).reshape(row_list, QUERY_HEADS, HEAD_SIZE), dk_part.transpose(1, 0, 2), dv_part.transpose(1, 0, 2))

def round_remote(part):
    narrow = lax.optimization_barrier(part[:WINDOW_KEYS].astype(jnp.bfloat16))
    return jnp.concatenate([narrow.astype(jnp.float32), part[WINDOW_KEYS:]], axis=0)

def reference(queries, raw_key_rows, values, out_grad, query_gain, key_norm_gain):

    def one_sequence(operands):
        query_seq, key_sequence, value_sequence, grad_seq = operands
        token_positions = jnp.arange(TOKEN_COUNT, dtype=jnp.int32)
        query_prep, query_back = jax.vjp(lambda input_arrays: prepare_inputs(input_arrays, query_gain, token_positions), query_seq.astype(jnp.float32).reshape(TOKEN_COUNT, QUERY_HEADS, HEAD_SIZE))
        key_prepared, key_backward = jax.vjp(lambda input_arrays: prepare_inputs(input_arrays, key_norm_gain, token_positions), key_sequence.astype(jnp.float32).reshape(TOKEN_COUNT, KEY_VALUE_HEADS, HEAD_SIZE))
        query_hat = query_prep.astype(jnp.bfloat16)
        key_normalized = key_prepared.astype(jnp.bfloat16)
        value_head_rows = value_sequence.reshape(TOKEN_COUNT, KEY_VALUE_HEADS, HEAD_SIZE)
        grad_heads = grad_seq.reshape(TOKEN_COUNT, QUERY_HEADS, HEAD_SIZE)
        padding_rows = jnp.zeros((WINDOW_KEYS, KEY_VALUE_HEADS, HEAD_SIZE), jnp.bfloat16)
        key_padded = jnp.concatenate([padding_rows, key_normalized], axis=0)
        value_padded = jnp.concatenate([padding_rows, value_head_rows], axis=0)
        span = WINDOW_KEYS + TOK_DEV

        def block(buffer_list, block_index):
            key_buf, value_buf = buffer_list
            anchor = block_index * TOK_DEV
            query_tile = lax.dynamic_slice_in_dim(query_hat, anchor, TOK_DEV, 0)
            gradient_block = lax.dynamic_slice_in_dim(grad_heads, anchor, TOK_DEV, 0)
            key_block = lax.dynamic_slice_in_dim(key_padded, anchor, span, 0)
            value_block = lax.dynamic_slice_in_dim(value_padded, anchor, span, 0)
            mask_table = visible(anchor, TOK_DEV, span)
            dq_part, dk_part, dv_part = head_terms(query_tile, key_block, value_block, gradient_block, mask_table)
            dk_part = round_remote(dk_part)
            dv_part = round_remote(dv_part)
            key_buf = lax.dynamic_update_slice_in_dim(key_buf, lax.dynamic_slice_in_dim(key_buf, anchor, span, 0) + dk_part, anchor, 0)
            value_buf = lax.dynamic_update_slice_in_dim(value_buf, lax.dynamic_slice_in_dim(value_buf, anchor, span, 0) + dv_part, anchor, 0)
            return ((key_buf, value_buf), dq_part)
        blank_start = jnp.zeros((WINDOW_KEYS + TOKEN_COUNT, KEY_VALUE_HEADS, HEAD_SIZE), jnp.float32)
        buffer_list, dq_blocks = lax.scan(block, (blank_start, blank_start), jnp.arange(N_SEQ, dtype=jnp.int32))
        dq_hat = dq_blocks.reshape(TOKEN_COUNT, QUERY_HEADS, HEAD_SIZE)
        query_grad = query_back(dq_hat)[0].astype(jnp.bfloat16).reshape(TOKEN_COUNT, QUERY_HEADS * HEAD_SIZE)
        key_gradient = key_backward(buffer_list[0][WINDOW_KEYS:])[0].astype(jnp.bfloat16).reshape(TOKEN_COUNT, KEY_VALUE_HEADS * HEAD_SIZE)
        value_gradient = buffer_list[1][WINDOW_KEYS:].astype(jnp.bfloat16).reshape(TOKEN_COUNT, KEY_VALUE_HEADS * HEAD_SIZE)
        return (query_grad, key_gradient, value_gradient)
    results = lax.map(one_sequence, (queries, raw_key_rows, values, out_grad))
    return (results[0], results[1], results[2])
```

```python
import functools

import jax
import jax.numpy as jnp
import numpy as np
from jax import lax
from jax.experimental import pallas as pl
from jax.experimental.pallas import tpu as pltpu
from jax.sharding import PartitionSpec as P

HEAD = 128
GROUP = 8
TOK = 128
SPAN = GROUP * TOK
WINDOW = 1024
SCALE = 168.0 ** (-0.5)
LOG2E = 1.4426950408889634
ROPE_BASE = 10000.0
EPSILON = 1e-06
NT = (((1,), (1,)), ((), ()))
NN = (((1,), (0,)), ((), ()))


def mm(a, b, dims):
    return lax.dot_general(a, b, dims, preferred_element_type=jnp.float32)


def inverse_norm(x):
    return lax.rsqrt(jnp.mean(x * x, axis=-1, keepdims=True) + EPSILON)


def rotate(n, cosine, sine):
    return n * cosine + pltpu.roll(n, HEAD // 2, 1) * sine


def prepare(x, gain, cosine, sine):
    return rotate(x * inverse_norm(x) * gain, cosine, sine)


def prepare_back(x, gain, cosine, sine, dy):
    inv = inverse_norm(x)
    h = (dy * cosine + pltpu.roll(dy * sine, HEAD // 2, 1)) * gain
    return inv * h - x * (inv * inv * inv * jnp.mean(x * h, axis=-1, keepdims=True))


def attend_kernel(
    low_ref, qd_ref, kv_ref, prev_ref, gain_ref, cos_ref, sin_ref,
    qg_ref, remote_ref, own_ref,
    k_s, kt_s, v_s, dk_s, dv_s,
):
    low = low_ref[0]
    q_gain = gain_ref[0:1, :]
    k_gain = gain_ref[1:2, :]

    def load_keys(i, _):
        for base, src in ((0, prev_ref), (SPAN, kv_ref)):
            rows = pl.ds(pl.multiple_of(i * TOK, TOK), TOK)
            at = pl.ds(pl.multiple_of(base + i * TOK, TOK), TOK)
            block = src[rows, :]
            hat = prepare(block[:, :HEAD].astype(jnp.float32), k_gain, cos_ref[at, :], sin_ref[at, :])
            k_s[at, :] = hat.astype(jnp.bfloat16)
            kt_s[:, at] = hat.T.astype(jnp.bfloat16)
            v_s[at, :] = block[:, HEAD:]
            dk_s[at, :] = jnp.zeros((TOK, HEAD), jnp.float32)
            dv_s[at, :] = jnp.zeros((TOK, HEAD), jnp.float32)
        return 0

    lax.fori_loop(0, GROUP, load_keys, 0)

    wide = WINDOW + TOK

    def step(b, _):
        rows = pl.ds(pl.multiple_of(b * TOK, TOK), TOK)
        at = pl.ds(pl.multiple_of(SPAN + b * TOK, TOK), TOK)
        keys = pl.ds(pl.multiple_of(b * TOK, TOK), wide)
        cosine, sine = cos_ref[at, :], sin_ref[at, :]
        raw = [qd_ref[rows, h * HEAD : (h + 1) * HEAD].astype(jnp.float32) for h in range(2)]
        q = jnp.concatenate([prepare(x, q_gain, cosine, sine) for x in raw], axis=0).astype(jnp.bfloat16)
        do = jnp.concatenate(
            [qd_ref[rows, (2 + h) * HEAD : (3 + h) * HEAD] for h in range(2)], axis=0
        )
        s = mm(k_s[keys, :], q, NT)
        row = lax.broadcasted_iota(jnp.int32, (wide, 2 * TOK), 0)
        col = lax.broadcasted_iota(jnp.int32, (wide, 2 * TOK), 1) % TOK
        seen = (row > col) & (row <= col + WINDOW) & (row >= low - b * TOK)
        s = jnp.where(seen, s * (SCALE * LOG2E), -1e30)
        w = jnp.exp2(s - jnp.max(s, axis=0, keepdims=True))
        probs = w * (1.0 / jnp.sum(w, axis=0, keepdims=True))
        pb = probs.astype(jnp.bfloat16)
        dp = mm(v_s[keys, :], do, NT)
        delta = jnp.sum(pb.astype(jnp.float32) * dp, axis=0, keepdims=True)
        ds = (probs * (dp - delta)).astype(jnp.bfloat16)
        dv_s[keys, :] += mm(pb, do, NN)
        dk_s[keys, :] += mm(ds, q, NN)
        dq = (mm(kt_s[:, keys], ds, NN) * SCALE).T
        for h in range(2):
            back = prepare_back(raw[h], q_gain, cosine, sine, dq[h * TOK : (h + 1) * TOK, :])
            qg_ref[rows, h * HEAD : (h + 1) * HEAD] = back.astype(jnp.bfloat16)
        return 0

    lax.fori_loop(0, GROUP, step, 0)

    remote_ref[:, :HEAD] = (dk_s[:SPAN, :] * SCALE).astype(jnp.bfloat16)
    remote_ref[:, HEAD:] = dv_s[:SPAN, :].astype(jnp.bfloat16)
    own_ref[:, :HEAD] = dk_s[SPAN:, :] * SCALE
    own_ref[:, HEAD:] = dv_s[SPAN:, :]


def finish_kernel(own_ref, back_ref, kv_ref, gain_ref, cos_ref, sin_ref, out_ref):
    total = own_ref[...] + back_ref[...].astype(jnp.float32)
    raw = kv_ref[:, :HEAD].astype(jnp.float32)
    dk = prepare_back(raw, gain_ref[1:2, :], cos_ref[...], sin_ref[...], total[:, :HEAD])
    out_ref[:, :HEAD] = dk.astype(jnp.bfloat16)
    out_ref[:, HEAD:] = total[:, HEAD:].astype(jnp.bfloat16)


VM = pl.BlockSpec(memory_space=pltpu.VMEM)
SM = pl.BlockSpec(memory_space=pltpu.SMEM)


def routes(mesh):
    n_seq = mesh.shape["seq"]
    groups = n_seq // GROUP

    def device(x, z, low):
        return (z % 8) * n_seq + (x * 2 + z // 8) * GROUP + low

    plan = {}
    for sign in (1, -1):
        first, second = [], []
        for x in range(groups // 2):
            for z in range(16):
                if x * 2 + z // 8 + 1 == groups:
                    continue
                mid = (z + 4 * sign) % 16
                end = (z + 8) % 16
                for low in range(GROUP):
                    first.append((device(x, z, low), device(x, mid, low)))
                    second.append((device(x, mid, low), device(x + z // 8, end, low)))
        plan[sign] = (first, second)
    return plan


def carry(block, plan, back):
    half = block.shape[0] // 2
    parts = []
    for sign, part in ((1, block[:half]), (-1, block[half:])):
        legs = plan[sign]
        if back:
            legs = [[(b, a) for a, b in leg] for leg in legs[::-1]]
        for leg in legs:
            part = lax.ppermute(part, ("dp", "seq"), leg)
        parts.append(part)
    return jnp.concatenate(parts, axis=0)


def body(plan, n_seq, queries, raw_key_rows, values, out_grad, query_gain, key_norm_gain):
    members = [[g * GROUP + i for i in range(GROUP)] for g in range(n_seq // GROUP)]
    swap = functools.partial(
        lax.all_to_all, axis_name="seq", split_axis=0, concat_axis=0, axis_index_groups=members
    )

    def by_head(x):
        return x[0].reshape(TOK, GROUP, -1).transpose(1, 0, 2)

    kv = swap(jnp.concatenate([by_head(raw_key_rows), by_head(values)], axis=-1))
    kv = kv.reshape(SPAN, 2 * HEAD)
    prev = carry(kv, plan, False)
    qd = swap(jnp.concatenate([by_head(queries), by_head(out_grad)], axis=-1))
    qd = qd.reshape(SPAN, 4 * HEAD)

    dp = lax.axis_index("dp")
    n_dp = lax.axis_size("dp")
    part = jnp.stack([query_gain, key_norm_gain])
    gains = lax.dynamic_update_slice(jnp.zeros((2, HEAD), jnp.float32), part, (0, dp * part.shape[1]))
    for bit in (1, 2, 4):
        gains = gains + lax.ppermute(gains, "dp", [(i, i ^ bit) for i in range(n_dp)])

    group = lax.axis_index("seq") // GROUP
    positions = (group - 1) * SPAN + jnp.arange(2 * SPAN, dtype=jnp.int32)
    frequency = ROPE_BASE ** (-jnp.arange(HEAD // 2).astype(jnp.float32) * (2.0 / HEAD))
    angles = positions.astype(jnp.float32)[:, None] * frequency[None, :]
    cosine, sine = jnp.cos(angles), jnp.sin(angles)
    cosine = jnp.concatenate([cosine, cosine], axis=-1)
    sine = jnp.concatenate([-sine, sine], axis=-1)
    low = jnp.where(group == 0, SPAN, 0).astype(jnp.int32).reshape(1)

    qg, remote, own = pl.pallas_call(
        attend_kernel,
        out_shape=(
            jax.ShapeDtypeStruct((SPAN, 2 * HEAD), jnp.bfloat16),
            jax.ShapeDtypeStruct((SPAN, 2 * HEAD), jnp.bfloat16),
            jax.ShapeDtypeStruct((SPAN, 2 * HEAD), jnp.float32),
        ),
        in_specs=[SM] + [VM] * 6,
        out_specs=(VM, VM, VM),
        scratch_shapes=[
            pltpu.VMEM((2 * SPAN, HEAD), jnp.bfloat16),
            pltpu.VMEM((HEAD, 2 * SPAN), jnp.bfloat16),
            pltpu.VMEM((2 * SPAN, HEAD), jnp.bfloat16),
            pltpu.VMEM((2 * SPAN, HEAD), jnp.float32),
            pltpu.VMEM((2 * SPAN, HEAD), jnp.float32),
        ],
        cost_estimate=pl.CostEstimate(flops=4 * 10**9, bytes_accessed=8 * 2**20, transcendentals=2 * 10**6),
        name="attend",
    )(low, qd, kv, prev, gains, cosine, sine)

    back = carry(remote, plan, True)
    qg = swap(qg.reshape(GROUP, TOK, 2 * HEAD))
    kvg = pl.pallas_call(
        finish_kernel,
        out_shape=jax.ShapeDtypeStruct((SPAN, 2 * HEAD), jnp.bfloat16),
        in_specs=[VM] * 6,
        out_specs=VM,
        name="finish",
    )(own, back, kv, gains, cosine[SPAN:], sine[SPAN:])
    kvg = swap(kvg.reshape(GROUP, TOK, 2 * HEAD))

    def by_token(x):
        return x.transpose(1, 0, 2).reshape(1, TOK, -1)

    return by_token(qg), by_token(kvg[:, :, :HEAD]), by_token(kvg[:, :, HEAD:])


def solution(mesh):
    spec = P("dp", "seq", None)
    return jax.shard_map(
        functools.partial(body, routes(mesh), mesh.shape["seq"]),
        mesh=mesh,
        in_specs=(spec, spec, spec, spec, P("dp"), P("dp")),
        out_specs=(spec, spec, spec),
        check_vma=False,
    )
```

```python
import functools

import jax
import jax.numpy as jnp
import numpy as np
from jax import lax
from jax.experimental import pallas as pl
from jax.experimental.pallas import tpu as pltpu
from jax.sharding import PartitionSpec as P

HEAD = 128
GROUP = 8
TOK = 128
SPAN = GROUP * TOK
WINDOW = 1024
SCALE = 168.0 ** (-0.5)
LOG2E = 1.4426950408889634
ROPE_BASE = 10000.0
EPSILON = 1e-06
NT = (((1,), (1,)), ((), ()))
NN = (((1,), (0,)), ((), ()))
MESH = pl.DeviceIdType.MESH
BF16 = jnp.bfloat16
F32 = jnp.float32


def mm(a, b, dims):
    return lax.dot_general(a, b, dims, preferred_element_type=F32)


def inverse_norm(x):
    return lax.rsqrt(jnp.mean(x * x, axis=-1, keepdims=True) + EPSILON)


def prepare(x, gain, cosine, sine):
    n = x * inverse_norm(x) * gain
    return n * cosine + pltpu.roll(n, HEAD // 2, 1) * sine


def prepare_back(x, gain, cosine, sine, dy):
    inv = inverse_norm(x)
    h = (dy * cosine + pltpu.roll(dy * sine, HEAD // 2, 1)) * gain
    return inv * h - x * (inv * inv * inv * jnp.mean(x * h, axis=-1, keepdims=True))


def block(i, base=0):
    return pl.ds(pl.multiple_of(base + i * TOK, TOK), TOK)


def lanes(i, width):
    return pl.ds(pl.multiple_of(i * width, width), width)


def layer_kernel(
    q_in, k_in, v_in, do_in, gain_in, cos_in, sin_in,
    oq, ok, ov,
    land, qd, gain_s, cos_s, sin_s, k_s, kt_s, dk_s, dv_s,
    relay_f, relay_b, ret_s, ret_l, qg_s, kvg_s, lq, lk, lv,
    in_send, in_recv, gain_send, gain_recv, z_send, z_recv, out_send, out_recv, self_sem,
):
    d = lax.axis_index("dp")
    seq = lax.axis_index("seq")
    r = lax.rem(seq, GROUP)
    g = lax.div(seq, GROUP)
    n_g = lax.div(lax.axis_size("seq"), GROUP)
    n_x = n_g // 2
    x = lax.div(g, 2)
    z = lax.rem(g, 2) * 8 + d
    low = jnp.where(g == 0, SPAN, 0)

    def mate(p):
        return (d, g * GROUP + p)

    def place(px, pz):
        return (lax.rem(pz, 8), (px * 2 + lax.div(pz, 8)) * GROUP + r)

    def up(sign):
        return lax.rem(z + 4 * sign + 16, 16)

    def remote(src, dst, send, recv, device):
        return pltpu.make_async_remote_copy(
            src_ref=src, dst_ref=dst, send_sem=send, recv_sem=recv, device_id=device, device_id_type=MESH
        )

    barrier = pltpu.get_barrier_semaphore()

    def greet(device):
        pl.semaphore_signal(barrier, inc=1, device_id=device, device_id_type=MESH)

    for k in range(1, GROUP):
        greet(mate(lax.rem(r + k, GROUP)))
    for k in range(1, 8):
        greet((lax.rem(d + k, 8), seq))
    for dx in (-1, 0, 1):
        for hi in (0, 1):
            greet((lax.rem(d + 4, 8), (lax.rem(x + dx + n_x, n_x) * 2 + hi) * GROUP + r))
    pl.semaphore_wait(barrier, 20)

    kinds = (
        (k_in, HEAD, land, SPAN, 0),
        (v_in, HEAD, land, SPAN, HEAD),
        (q_in, 2 * HEAD, qd, 0, 0),
        (do_in, 2 * HEAD, qd, 0, 2 * HEAD),
    )

    def into(kind, k):
        src, width, dst, base, at = kinds[kind]
        p = lax.rem(r + k, GROUP)
        return remote(
            src.at[0, :, lanes(p, width)], dst.at[block(r, base), at : at + width],
            in_send.at[kind, k], in_recv.at[kind, k], mate(p),
        )

    def keep(kind):
        src, width, dst, base, at = kinds[kind]
        return pltpu.make_async_copy(
            src.at[0, :, lanes(r, width)], dst.at[block(r, base), at : at + width], self_sem.at[kind]
        )

    def share(k):
        return remote(
            gain_in, gain_s.at[k], gain_send.at[k], gain_recv.at[k], (lax.rem(d + k, 8), seq)
        )

    for kind in (0, 1):
        keep(kind).start()
    for k in range(1, GROUP):
        for kind in (0, 1):
            into(kind, k).start()
    for k in range(1, 8):
        share(k).start()
    for kind in (2, 3):
        keep(kind).start()
    for k in range(1, GROUP):
        for kind in (2, 3):
            into(kind, k).start()

    def chunk(c):
        return lax.rem(r - c + GROUP, GROUP)

    def leg0(c):
        return remote(
            land.at[block(chunk(c), SPAN), :], relay_f.at[c],
            z_send.at[0, c], z_recv.at[0, c], place(x, up(1 - 2 * (c % 2))),
        )

    def leg1(c):
        sign = 1 - 2 * (c % 2)
        return remote(
            relay_f.at[c], land.at[block(chunk(c)), :],
            z_send.at[1, c], z_recv.at[1, c],
            place(lax.rem(x + lax.div(up(-sign), 8), n_x), up(sign)),
        )

    def leg2(c):
        sign = 1 - 2 * (c % 2)
        return remote(
            ret_s.at[block(c), :], relay_b.at[c],
            z_send.at[2, c], z_recv.at[2, c],
            place(lax.rem(x + n_x - 1 + lax.div(z, 8), n_x), up(-sign)),
        )

    def leg3(c):
        sign = 1 - 2 * (c % 2)
        return remote(
            relay_b.at[c], ret_l.at[block(c), :],
            z_send.at[3, c], z_recv.at[3, c], place(x, up(-sign)),
        )

    for c in range(GROUP):
        for kind in (0, 1):
            if c == 0:
                keep(kind).wait()
            else:
                into(kind, c).wait_recv()
        leg0(c).start()

    gains = gain_in[...]
    for k in range(1, 8):
        share(k).wait_recv()
        gains = gains + gain_s[k]
    q_gain, k_gain = gains[0:1, :], gains[1:2, :]

    def hat(at):
        raw = land[at, :HEAD].astype(F32)
        key = prepare(raw, k_gain, cos_s[at, :], sin_s[at, :])
        k_s[at, :] = key.astype(BF16)
        kt_s[:, at] = key.T.astype(BF16)

    cos_t, sin_t = cos_in[16:, :], sin_in[16:, :]

    def tables(i, _):
        cos_b, sin_b = cos_in[pl.ds(i, 1), :], sin_in[pl.ds(i, 1), :]
        cos_s[block(i), :] = cos_b * cos_t - sin_b * sin_t
        sin_s[block(i), :] = sin_b * cos_t + cos_b * sin_t
        dk_s[block(i), :] = jnp.zeros((TOK, HEAD), F32)
        dv_s[block(i), :] = jnp.zeros((TOK, HEAD), F32)
        return 0

    lax.fori_loop(0, 2 * GROUP, tables, 0)

    def own_keys(i, _):
        hat(block(i, SPAN))
        return 0

    lax.fori_loop(0, GROUP, own_keys, 0)

    for c in range(GROUP):
        leg0(c).wait_recv()
        leg1(c).start()
    for kind in (2, 3):
        keep(kind).wait()
        for k in range(1, GROUP):
            into(kind, k).wait_recv()

    def previous_keys(c, _):
        leg1(c).wait_recv()
        hat(block(chunk(c)))
        return 0

    lax.fori_loop(0, GROUP, previous_keys, 0)

    outs = ((qg_s, 0, 2 * HEAD, lq), (kvg_s, 0, HEAD, lk), (kvg_s, HEAD, HEAD, lv))

    def send_out(kind, p):
        src, at, width, dst = outs[kind]
        return remote(
            src.at[block(p), at : at + width], dst.at[:, lanes(r, width)],
            out_send.at[kind, p], out_recv.at[kind, r], mate(p),
        )

    def keep_out(kind):
        src, at, width, dst = outs[kind]
        return pltpu.make_async_copy(
            src.at[block(r), at : at + width], dst.at[:, lanes(r, width)], self_sem.at[4 + kind]
        )

    def arrive_out(kind, p):
        src, at, width, dst = outs[kind]
        return remote(
            src.at[block(p), at : at + width], dst.at[:, lanes(p, width)],
            out_send.at[kind, p], out_recv.at[kind, p], mate(p),
        )

    def deliver(kind, p):
        @pl.when(p != r)
        def _():
            send_out(kind, p).start()

        @pl.when(p == r)
        def _():
            keep_out(kind).start()

    wide = WINDOW + TOK

    def step(b, _):
        rows, keys = block(b), pl.ds(pl.multiple_of(b * TOK, TOK), wide)
        cosine, sine = cos_s[block(b, SPAN), :], sin_s[block(b, SPAN), :]
        raw = [qd[rows, h * HEAD : (h + 1) * HEAD].astype(F32) for h in range(2)]
        q = jnp.concatenate([prepare(v, q_gain, cosine, sine) for v in raw], axis=0).astype(BF16)
        do = jnp.concatenate([qd[rows, (2 + h) * HEAD : (3 + h) * HEAD] for h in range(2)], axis=0)
        s = mm(k_s[keys, :], q, NT)
        row = lax.broadcasted_iota(jnp.int32, (wide, 2 * TOK), 0)
        col = lax.broadcasted_iota(jnp.int32, (wide, 2 * TOK), 1) % TOK
        seen = (row > col) & (row <= col + WINDOW) & (row >= low - b * TOK)
        s = jnp.where(seen, s * (SCALE * LOG2E), -1e30)
        w = jnp.exp2(s - jnp.max(s, axis=0, keepdims=True))
        probs = w * (1.0 / jnp.sum(w, axis=0, keepdims=True))
        pb = probs.astype(BF16)
        dp = mm(land[keys, HEAD:], do, NT)
        delta = jnp.sum(pb.astype(F32) * dp, axis=0, keepdims=True)
        ds = (probs * (dp - delta)).astype(BF16)
        dv_s[keys, :] += mm(pb, do, NN)
        dk_s[keys, :] += mm(ds, q, NN)
        ret_s[rows, :HEAD] = (dk_s[rows, :] * SCALE).astype(BF16)
        ret_s[rows, HEAD:] = dv_s[rows, :].astype(BF16)
        leg2(b).start()
        dq = (mm(kt_s[:, keys], ds, NN) * SCALE).T
        for h in range(2):
            back = prepare_back(raw[h], q_gain, cosine, sine, dq[h * TOK : (h + 1) * TOK, :])
            qg_s[rows, h * HEAD : (h + 1) * HEAD] = back.astype(BF16)

        @pl.when(b >= 2)
        def _():
            leg2(b - 2).wait_recv()
            leg3(b - 2).start()

        deliver(0, b)
        return 0

    lax.fori_loop(0, GROUP, step, 0)
    for c in (GROUP - 2, GROUP - 1):
        leg2(c).wait_recv()
        leg3(c).start()

    def finish(b, _):
        rows, at = block(b), block(b, SPAN)
        leg3(b).wait_recv()
        dk = dk_s[at, :] * SCALE + ret_l[rows, :HEAD].astype(F32)
        back = prepare_back(land[at, :HEAD].astype(F32), k_gain, cos_s[at, :], sin_s[at, :], dk)
        kvg_s[rows, :HEAD] = back.astype(BF16)
        kvg_s[rows, HEAD:] = (dv_s[at, :] + ret_l[rows, HEAD:].astype(F32)).astype(BF16)
        deliver(1, b)
        deliver(2, b)
        return 0

    lax.fori_loop(0, GROUP, finish, 0)

    for k in range(1, GROUP):
        for kind in range(4):
            into(kind, k).wait_send()
        share(k).wait_send()
    for c in range(GROUP):
        for leg in (leg0, leg1, leg2, leg3):
            leg(c).wait_send()
    for kind, result in ((0, oq), (1, ok), (2, ov)):
        for k in range(1, GROUP):
            p = lax.rem(r + k, GROUP)
            arrive_out(kind, p).wait_recv()
            send_out(kind, p).wait_send()
        keep_out(kind).wait()
        result[0] = outs[kind][3][...]


def body(queries, raw_key_rows, values, out_grad, query_gain, key_norm_gain):
    dp = lax.axis_index("dp")
    part = jnp.stack([query_gain, key_norm_gain])
    gains = lax.dynamic_update_slice(jnp.zeros((8, HEAD), F32), part, (0, dp * part.shape[1]))
    group = lax.axis_index("seq") // GROUP
    index = jnp.arange(16 + TOK, dtype=jnp.int32)
    positions = jnp.where(index < 16, (group - 1) * SPAN + index * TOK, index - 16).astype(F32)
    half = np.arange(HEAD) % (HEAD // 2)
    frequency = jnp.asarray((ROPE_BASE ** (-half * (2.0 / HEAD))).astype(np.float32))
    sign = jnp.asarray(np.where(np.arange(HEAD) < HEAD // 2, -1.0, 1.0).astype(np.float32))
    angles = positions[:, None] * frequency[None, :]
    anywhere = pl.BlockSpec(memory_space=pl.ANY)
    vmem = pl.BlockSpec(memory_space=pltpu.VMEM)
    dma = pltpu.SemaphoreType.DMA
    return pl.pallas_call(
        layer_kernel,
        out_shape=tuple(
            jax.ShapeDtypeStruct(a.shape, BF16) for a in (queries, raw_key_rows, values)
        ),
        in_specs=[anywhere] * 4 + [vmem] * 3,
        out_specs=(vmem, vmem, vmem),
        scratch_shapes=[
            pltpu.VMEM((2 * SPAN, 2 * HEAD), BF16),
            pltpu.VMEM((SPAN, 4 * HEAD), BF16),
            pltpu.VMEM((8, 8, HEAD), F32),
            pltpu.VMEM((2 * SPAN, HEAD), F32),
            pltpu.VMEM((2 * SPAN, HEAD), F32),
            pltpu.VMEM((2 * SPAN, HEAD), BF16),
            pltpu.VMEM((HEAD, 2 * SPAN), BF16),
            pltpu.VMEM((2 * SPAN, HEAD), F32),
            pltpu.VMEM((2 * SPAN, HEAD), F32),
            pltpu.VMEM((GROUP, TOK, 2 * HEAD), BF16),
            pltpu.VMEM((GROUP, TOK, 2 * HEAD), BF16),
            pltpu.VMEM((SPAN, 2 * HEAD), BF16),
            pltpu.VMEM((SPAN, 2 * HEAD), BF16),
            pltpu.VMEM((SPAN, 2 * HEAD), BF16),
            pltpu.VMEM((SPAN, 2 * HEAD), BF16),
            pltpu.VMEM((TOK, 2 * SPAN), BF16),
            pltpu.VMEM((TOK, SPAN), BF16),
            pltpu.VMEM((TOK, SPAN), BF16),
            dma((4, 8)), dma((4, 8)), dma((8,)), dma((8,)),
            dma((4, 8)), dma((4, 8)), dma((3, 8)), dma((3, 8)), dma((7,)),
        ],
        compiler_params=pltpu.CompilerParams(collective_id=0, has_side_effects=True),
        name="layer_backward",
    )(
        queries, raw_key_rows, values, out_grad, gains,
        jnp.cos(angles), jnp.sin(angles) * sign[None, :],
    )


def solution(mesh):
    spec = P("dp", "seq", None)
    return jax.shard_map(
        body,
        mesh=mesh,
        in_specs=(spec, spec, spec, spec, P("dp"), P("dp")),
        out_specs=(spec, spec, spec),
        check_vma=False,
    )
```

```python
import functools

import jax
import jax.numpy as jnp
import numpy as np
from jax import lax
from jax.experimental import pallas as pl
from jax.experimental.pallas import tpu as pltpu
from jax.sharding import PartitionSpec as P

HEAD = 128
GROUP = 8
TOK = 128
SPAN = GROUP * TOK
WINDOW = 1024
SCALE = 168.0 ** (-0.5)
LOG2E = 1.4426950408889634
ROPE_BASE = 10000.0
EPSILON = 1e-06
NT = (((1,), (1,)), ((), ()))
NN = (((1,), (0,)), ((), ()))
MESH = pl.DeviceIdType.MESH
BF16 = jnp.bfloat16
F32 = jnp.float32


def mm(a, b, dims):
    return lax.dot_general(a, b, dims, preferred_element_type=F32)


def inverse_norm(x):
    return lax.rsqrt(jnp.mean(x * x, axis=-1, keepdims=True) + EPSILON)


def prepare(x, gain, cosine, sine):
    n = x * inverse_norm(x) * gain
    return n * cosine + pltpu.roll(n, HEAD // 2, 1) * sine


def prepare_back(x, gain, cosine, sine, dy):
    inv = inverse_norm(x)
    h = (dy * cosine + pltpu.roll(dy * sine, HEAD // 2, 1)) * gain
    return inv * h - x * (inv * inv * inv * jnp.mean(x * h, axis=-1, keepdims=True))


def block(i, base=0):
    return pl.ds(pl.multiple_of(base + i * TOK, TOK), TOK)


def half(i, s, base=0):
    return pl.ds(pl.multiple_of(base + i * TOK + s * (TOK // 2), TOK // 2), TOK // 2)


def lanes(i, width):
    return pl.ds(pl.multiple_of(i * width, width), width)


def layer_kernel(
    q_in, k_in, v_in, do_in, gain_in, cos_in, sin_in,
    oq, ok, ov,
    land, qd, gain_s, cos_s, sin_s, k_s, kt_s, dk_s, dv_s,
    relay_f, relay_b, ret_s, ret_l, qg_s, kvg_s, lq, lk, lv,
    in_send, in_recv, gain_send, gain_recv, z_send, z_recv, out_send, out_recv, self_sem,
):
    d = lax.axis_index("dp")
    seq = lax.axis_index("seq")
    r = lax.rem(seq, GROUP)
    g = lax.div(seq, GROUP)
    n_g = lax.div(lax.axis_size("seq"), GROUP)
    n_x = n_g // 2
    x = lax.div(g, 2)
    z = lax.rem(g, 2) * 8 + d
    low = jnp.where(g == 0, SPAN, 0)

    def mate(p):
        return (d, g * GROUP + p)

    def place(px, pz):
        return (lax.rem(pz, 8), (px * 2 + lax.div(pz, 8)) * GROUP + r)

    def up(sign):
        return lax.rem(z + 4 * sign + 16, 16)

    def remote(src, dst, send, recv, device):
        return pltpu.make_async_remote_copy(
            src_ref=src, dst_ref=dst, send_sem=send, recv_sem=recv, device_id=device, device_id_type=MESH
        )

    barrier = pltpu.get_barrier_semaphore()

    def greet(device):
        pl.semaphore_signal(barrier, inc=1, device_id=device, device_id_type=MESH)

    for k in range(1, GROUP):
        greet(mate(lax.rem(r + k, GROUP)))
    for k in range(1, 8):
        greet((lax.rem(d + k, 8), seq))
    for dx in (-1, 0, 1):
        for hi in (0, 1):
            greet((lax.rem(d + 4, 8), (lax.rem(x + dx + n_x, n_x) * 2 + hi) * GROUP + r))
    pl.semaphore_wait(barrier, 20)

    kinds = (
        (k_in, HEAD, land, SPAN, 0),
        (v_in, HEAD, land, SPAN, HEAD),
        (q_in, 2 * HEAD, qd, 0, 0),
        (do_in, 2 * HEAD, qd, 0, 2 * HEAD),
    )

    def into(kind, k):
        src, width, dst, base, at = kinds[kind]
        p = lax.rem(r + k, GROUP)
        return remote(
            src.at[0, :, lanes(p, width)], dst.at[block(r, base), at : at + width],
            in_send.at[kind, k], in_recv.at[kind, k], mate(p),
        )

    def keep(kind):
        src, width, dst, base, at = kinds[kind]
        return pltpu.make_async_copy(
            src.at[0, :, lanes(r, width)], dst.at[block(r, base), at : at + width], self_sem.at[kind]
        )

    def share(k):
        return remote(
            gain_in, gain_s.at[k], gain_send.at[k], gain_recv.at[k], (lax.rem(d + k, 8), seq)
        )

    for kind in (0, 1):
        keep(kind).start()
    for k in range(1, GROUP):
        for kind in (0, 1):
            into(kind, k).start()
    for k in range(1, 8):
        share(k).start()
    def chunk(c):
        return lax.rem(r - c + GROUP, GROUP)

    def hop(leg, c, s, src, dst, device):
        return remote(src, dst, z_send.at[leg, s, c], z_recv.at[leg, s, c], device)

    def leg0(c, s):
        return hop(0, c, s, land.at[half(chunk(c), s, SPAN), :], relay_f.at[half(c, s), :], place(x, up(1 - 2 * s)))

    def leg1(c, s):
        sign = 1 - 2 * s
        to = place(lax.rem(x + lax.div(up(-sign), 8), n_x), up(sign))
        return hop(1, c, s, relay_f.at[half(c, s), :], land.at[half(chunk(c), s), :], to)

    def leg2(c, s):
        to = place(lax.rem(x + n_x - 1 + lax.div(z, 8), n_x), up(2 * s - 1))
        return hop(2, c, s, ret_s.at[half(c, s), :], relay_b.at[half(c, s), :], to)

    def leg3(c, s):
        return hop(3, c, s, relay_b.at[half(c, s), :], ret_l.at[half(c, s), :], place(x, up(2 * s - 1)))

    def start(leg, c):
        for s in (0, 1):
            leg(c, s).start()

    def arrive(leg, c):
        for s in (0, 1):
            leg(c, s).wait_recv()

    def forward(first, second, c):
        for s in (0, 1):
            first(c, s).wait_recv()
            second(c, s).start()

    for c in range(GROUP):
        for kind in (0, 1):
            if c == 0:
                keep(kind).wait()
            else:
                into(kind, c).wait_recv()
        start(leg0, c)

    for kind in (2, 3):
        keep(kind).start()
    for k in range(1, GROUP):
        for kind in (2, 3):
            into(kind, k).start()

    gains = gain_in[...]
    for k in range(1, 8):
        share(k).wait_recv()
        gains = gains + gain_s[k]
    q_gain, k_gain = gains[0:1, :], gains[1:2, :]

    def hat(at):
        raw = land[at, :HEAD].astype(F32)
        key = prepare(raw, k_gain, cos_s[at, :], sin_s[at, :])
        k_s[at, :] = key.astype(BF16)
        kt_s[:, at] = key.T.astype(BF16)

    cos_t, sin_t = cos_in[16:, :], sin_in[16:, :]

    def table(at, i):
        cos_b, sin_b = cos_in[pl.ds(i, 1), :], sin_in[pl.ds(i, 1), :]
        cos_s[at, :] = cos_b * cos_t - sin_b * sin_t
        sin_s[at, :] = sin_b * cos_t + cos_b * sin_t
        dk_s[at, :] = jnp.zeros((TOK, HEAD), F32)
        dv_s[at, :] = jnp.zeros((TOK, HEAD), F32)

    def first_half(c, _):
        forward(leg0, leg1, c)
        table(block(c), c)
        table(block(c, SPAN), c + GROUP)
        hat(block(c, SPAN))
        return 0

    lax.fori_loop(0, GROUP, first_half, 0)

    for kind in (2, 3):
        keep(kind).wait()
        for k in range(1, GROUP):
            into(kind, k).wait_recv()

    def previous_keys(c, _):
        arrive(leg1, c)
        hat(block(chunk(c)))
        return 0

    lax.fori_loop(0, GROUP, previous_keys, 0)

    outs = ((qg_s, 0, 2 * HEAD, lq), (kvg_s, 0, HEAD, lk), (kvg_s, HEAD, HEAD, lv))

    def send_out(kind, p):
        src, at, width, dst = outs[kind]
        return remote(
            src.at[block(p), at : at + width], dst.at[:, lanes(r, width)],
            out_send.at[kind, p], out_recv.at[kind, r], mate(p),
        )

    def keep_out(kind):
        src, at, width, dst = outs[kind]
        return pltpu.make_async_copy(
            src.at[block(r), at : at + width], dst.at[:, lanes(r, width)], self_sem.at[4 + kind]
        )

    def arrive_out(kind, p):
        src, at, width, dst = outs[kind]
        return remote(
            src.at[block(p), at : at + width], dst.at[:, lanes(p, width)],
            out_send.at[kind, p], out_recv.at[kind, p], mate(p),
        )

    def deliver(kind, p):
        @pl.when(p != r)
        def _():
            send_out(kind, p).start()

        @pl.when(p == r)
        def _():
            keep_out(kind).start()

    wide = WINDOW + TOK

    def step(b, _):
        rows, keys = block(b), pl.ds(pl.multiple_of(b * TOK, TOK), wide)
        cosine, sine = cos_s[block(b, SPAN), :], sin_s[block(b, SPAN), :]
        raw = [qd[rows, h * HEAD : (h + 1) * HEAD].astype(F32) for h in range(2)]
        q = jnp.concatenate([prepare(v, q_gain, cosine, sine) for v in raw], axis=0).astype(BF16)
        do = jnp.concatenate([qd[rows, (2 + h) * HEAD : (3 + h) * HEAD] for h in range(2)], axis=0)
        s = mm(k_s[keys, :], q, NT)
        row = lax.broadcasted_iota(jnp.int32, (wide, 2 * TOK), 0)
        col = lax.broadcasted_iota(jnp.int32, (wide, 2 * TOK), 1) % TOK
        seen = (row > col) & (row <= col + WINDOW) & (row >= low - b * TOK)
        s = jnp.where(seen, s * (SCALE * LOG2E), -1e30)
        w = jnp.exp2(s - jnp.max(s, axis=0, keepdims=True))
        probs = w * (1.0 / jnp.sum(w, axis=0, keepdims=True))
        pb = probs.astype(BF16)
        dp = mm(land[keys, HEAD:], do, NT)
        delta = jnp.sum(pb.astype(F32) * dp, axis=0, keepdims=True)
        ds = (probs * (dp - delta)).astype(BF16)
        dv_s[keys, :] += mm(pb, do, NN)
        dk_s[keys, :] += mm(ds, q, NN)
        ret_s[rows, :HEAD] = (dk_s[rows, :] * SCALE).astype(BF16)
        ret_s[rows, HEAD:] = dv_s[rows, :].astype(BF16)
        start(leg2, b)
        dq = (mm(kt_s[:, keys], ds, NN) * SCALE).T
        for h in range(2):
            back = prepare_back(raw[h], q_gain, cosine, sine, dq[h * TOK : (h + 1) * TOK, :])
            qg_s[rows, h * HEAD : (h + 1) * HEAD] = back.astype(BF16)

        @pl.when(b >= 2)
        def _():
            forward(leg2, leg3, b - 2)

        deliver(0, b)
        return 0

    lax.fori_loop(0, GROUP, step, 0)
    for c in (GROUP - 2, GROUP - 1):
        forward(leg2, leg3, c)

    def finish(b, _):
        rows, at = block(b), block(b, SPAN)
        arrive(leg3, b)
        dk = dk_s[at, :] * SCALE + ret_l[rows, :HEAD].astype(F32)
        back = prepare_back(land[at, :HEAD].astype(F32), k_gain, cos_s[at, :], sin_s[at, :], dk)
        kvg_s[rows, :HEAD] = back.astype(BF16)
        kvg_s[rows, HEAD:] = (dv_s[at, :] + ret_l[rows, HEAD:].astype(F32)).astype(BF16)
        deliver(1, b)
        deliver(2, b)
        return 0

    lax.fori_loop(0, GROUP, finish, 0)

    for k in range(1, GROUP):
        for kind in range(4):
            into(kind, k).wait_send()
        share(k).wait_send()
    for c in range(GROUP):
        for leg in (leg0, leg1, leg2, leg3):
            for s in (0, 1):
                leg(c, s).wait_send()
    for kind, result in ((0, oq), (1, ok), (2, ov)):
        for k in range(1, GROUP):
            p = lax.rem(r + k, GROUP)
            arrive_out(kind, p).wait_recv()
            send_out(kind, p).wait_send()
        keep_out(kind).wait()
        result[0] = outs[kind][3][...]


def settle_kernel(a, b, c, oa, ob, oc, sem):
    copies = [pltpu.make_async_copy(i, o, sem.at[n]) for n, (i, o) in enumerate(((a, oa), (b, ob), (c, oc)))]
    for copy in copies:
        copy.start()
    for copy in copies:
        copy.wait()


def body(queries, raw_key_rows, values, out_grad, query_gain, key_norm_gain):
    dp = lax.axis_index("dp")
    part = jnp.stack([query_gain, key_norm_gain])
    gains = lax.dynamic_update_slice(jnp.zeros((8, HEAD), F32), part, (0, dp * part.shape[1]))
    group = lax.axis_index("seq") // GROUP
    index = jnp.arange(16 + TOK, dtype=jnp.int32)
    positions = jnp.where(index < 16, (group - 1) * SPAN + index * TOK, index - 16).astype(F32)
    half = np.arange(HEAD) % (HEAD // 2)
    frequency = jnp.asarray((ROPE_BASE ** (-half * (2.0 / HEAD))).astype(np.float32))
    sign = jnp.asarray(np.where(np.arange(HEAD) < HEAD // 2, -1.0, 1.0).astype(np.float32))
    angles = positions[:, None] * frequency[None, :]
    anywhere = pl.BlockSpec(memory_space=pl.ANY)
    vmem = pl.BlockSpec(memory_space=pltpu.VMEM)
    dma = pltpu.SemaphoreType.DMA
    shapes = tuple(jax.ShapeDtypeStruct(a.shape, BF16) for a in (queries, raw_key_rows, values))
    grads = pl.pallas_call(
        layer_kernel,
        out_shape=shapes,
        in_specs=[anywhere] * 4 + [vmem] * 3,
        out_specs=(vmem, vmem, vmem),
        scratch_shapes=[
            pltpu.VMEM((2 * SPAN, 2 * HEAD), BF16),
            pltpu.VMEM((SPAN, 4 * HEAD), BF16),
            pltpu.VMEM((8, 8, HEAD), F32),
            pltpu.VMEM((2 * SPAN, HEAD), F32),
            pltpu.VMEM((2 * SPAN, HEAD), F32),
            pltpu.VMEM((2 * SPAN, HEAD), BF16),
            pltpu.VMEM((HEAD, 2 * SPAN), BF16),
            pltpu.VMEM((2 * SPAN, HEAD), F32),
            pltpu.VMEM((2 * SPAN, HEAD), F32),
            pltpu.VMEM((SPAN, 2 * HEAD), BF16),
            pltpu.VMEM((SPAN, 2 * HEAD), BF16),
            pltpu.VMEM((SPAN, 2 * HEAD), BF16),
            pltpu.VMEM((SPAN, 2 * HEAD), BF16),
            pltpu.VMEM((SPAN, 2 * HEAD), BF16),
            pltpu.VMEM((SPAN, 2 * HEAD), BF16),
            pltpu.VMEM((TOK, 2 * SPAN), BF16),
            pltpu.VMEM((TOK, SPAN), BF16),
            pltpu.VMEM((TOK, SPAN), BF16),
            dma((4, 8)), dma((4, 8)), dma((8,)), dma((8,)),
            dma((4, 2, 8)), dma((4, 2, 8)), dma((3, 8)), dma((3, 8)), dma((7,)),
        ],
        compiler_params=pltpu.CompilerParams(collective_id=0, has_side_effects=True),
        name="layer_backward",
    )(
        queries, raw_key_rows, values, out_grad, gains,
        jnp.cos(angles), jnp.sin(angles) * sign[None, :],
    )
    return pl.pallas_call(
        settle_kernel,
        out_shape=shapes,
        in_specs=[vmem] * 3,
        out_specs=(anywhere,) * 3,
        scratch_shapes=[dma((3,))],
        name="settle",
    )(*grads)


def solution(mesh):
    spec = P("dp", "seq", None)
    return jax.shard_map(
        body,
        mesh=mesh,
        in_specs=(spec, spec, spec, spec, P("dp"), P("dp")),
        out_specs=(spec, spec, spec),
        check_vma=False,
    )
```

```python
import functools

import jax
import jax.numpy as jnp
import numpy as np
from jax import lax
from jax.experimental import pallas as pl
from jax.experimental.pallas import tpu as pltpu
from jax.sharding import PartitionSpec as P

HEAD = 128
GROUP = 8
TOK = 128
SPAN = GROUP * TOK
WINDOW = 1024
SCALE = 168.0 ** (-0.5)
LOG2E = 1.4426950408889634
ROPE_BASE = 10000.0
EPSILON = 1e-06
NT = (((1,), (1,)), ((), ()))
NN = (((1,), (0,)), ((), ()))
MESH = pl.DeviceIdType.MESH
BF16 = jnp.bfloat16
F32 = jnp.float32


def mm(a, b, dims):
    return lax.dot_general(a, b, dims, preferred_element_type=F32)


def inverse_norm(x):
    return lax.rsqrt(jnp.mean(x * x, axis=-1, keepdims=True) + EPSILON)


def prepare(x, gain, cosine, sine):
    n = x * inverse_norm(x) * gain
    return n * cosine + pltpu.roll(n, HEAD // 2, 1) * sine


def prepare_back(x, gain, cosine, sine, dy):
    inv = inverse_norm(x)
    h = (dy * cosine + pltpu.roll(dy * sine, HEAD // 2, 1)) * gain
    return inv * h - x * (inv * inv * inv * jnp.mean(x * h, axis=-1, keepdims=True))


def block(i, base=0):
    return pl.ds(pl.multiple_of(base + i * TOK, TOK), TOK)


def half(i, s, base=0):
    return pl.ds(pl.multiple_of(base + i * TOK + s * (TOK // 2), TOK // 2), TOK // 2)


def lanes(i, width):
    return pl.ds(pl.multiple_of(i * width, width), width)


def layer_kernel(
    q_in, k_in, v_in, do_in, gain_in, cos_in, sin_in,
    oq, ok, ov,
    land, qd, gain_s, cos_s, sin_s, k_s, kt_s, dk_s, dv_s,
    relay_f, relay_b, ret_s, ret_l, qg_s, kvg_s, lq, lk, lv,
    in_send, in_recv, gain_send, gain_recv, z_send, z_recv, out_send, out_recv, self_sem,
):
    d = lax.axis_index("dp")
    seq = lax.axis_index("seq")
    r = lax.rem(seq, GROUP)
    g = lax.div(seq, GROUP)
    n_g = lax.div(lax.axis_size("seq"), GROUP)
    n_x = n_g // 2
    x = lax.div(g, 2)
    z = lax.rem(g, 2) * 8 + d
    low = jnp.where(g == 0, SPAN, 0)

    def mate(p):
        return (d, g * GROUP + p)

    out_far, back_far = 2 * n_x - 2 - 2 * x, 2 * x
    has_next, has_previous = (z < 8) | (x < n_x - 1), g > 0
    out_kind, back_kind = lax.div(z, 8), 1 - lax.div(z, 8)

    def wrap(v):
        return lax.rem(v + 32, 16)

    def place(px, pz):
        return (lax.rem(pz, 8), (lax.rem(px + n_x, n_x) * 2 + lax.div(pz, 8)) * GROUP + r)

    def remote(src, dst, send, recv, device):
        return pltpu.make_async_remote_copy(
            src_ref=src, dst_ref=dst, send_sem=send, recv_sem=recv, device_id=device, device_id_type=MESH
        )

    barrier = pltpu.get_barrier_semaphore()

    def greet(device):
        pl.semaphore_signal(barrier, inc=1, device_id=device, device_id_type=MESH)

    for k in range(1, GROUP):
        greet(mate(lax.rem(r + k, GROUP)))
    for k in range(1, 8):
        greet((lax.rem(d + k, 8), seq))
    for sign in (1, -1):
        greet(place(x, wrap(z + 4 * sign)))

        @pl.when(x < n_x - 1)
        def _():
            greet(place(x, wrap(z + out_far * sign)))
            greet(place(x + 1, wrap(z + out_far * sign)))
            greet(place(x + 1, wrap(z + (2 * x + 2) * sign)))

        @pl.when(x > 0)
        def _():
            greet(place(x, wrap(z + back_far * sign)))
            greet(place(x - 1, wrap(z + (2 * n_x - 2 * x) * sign)))
            greet(place(x - 1, wrap(z + back_far * sign)))

    pl.semaphore_wait(barrier, 16 + 6 * jnp.where(x < n_x - 1, 1, 0) + 6 * jnp.where(x > 0, 1, 0))

    kinds = (
        (k_in, HEAD, land, SPAN, 0),
        (v_in, HEAD, land, SPAN, HEAD),
        (q_in, 2 * HEAD, qd, 0, 0),
        (do_in, 2 * HEAD, qd, 0, 2 * HEAD),
    )

    def into(kind, k):
        src, width, dst, base, at = kinds[kind]
        p = lax.rem(r + k, GROUP)
        return remote(
            src.at[0, :, lanes(p, width)], dst.at[block(r, base), at : at + width],
            in_send.at[kind, k], in_recv.at[kind, k], mate(p),
        )

    def keep(kind):
        src, width, dst, base, at = kinds[kind]
        return pltpu.make_async_copy(
            src.at[0, :, lanes(r, width)], dst.at[block(r, base), at : at + width], self_sem.at[kind]
        )

    def share(k):
        return remote(
            gain_in, gain_s.at[k], gain_send.at[k], gain_recv.at[k], (lax.rem(d + k, 8), seq)
        )

    for kind in (0, 1):
        keep(kind).start()
    for k in range(1, GROUP):
        for kind in (0, 1):
            into(kind, k).start()
    for k in range(1, 8):
        share(k).start()
    def chunk(c):
        return lax.rem(r - c + GROUP, GROUP)

    def hop(leg, c, s, kind, end, src, dst, device):
        mark = c if end else c + kind * GROUP
        return remote(src, dst, z_send.at[leg, s, c + kind * GROUP], z_recv.at[leg, s, mark], device)

    def leg0(c, s, kind):
        to = place(x + kind, wrap(z + (4 + kind * (out_far - 4)) * (1 - 2 * s)))
        held = relay_f.at[half(c + kind * GROUP, s), :]
        return hop(0, c, s, kind, False, land.at[half(chunk(c), s, SPAN), :], held, to)

    def leg1(c, s, kind):
        sign = 1 - 2 * s
        to = place(x, wrap(z + (back_far if kind else 4) * sign))
        held = relay_f.at[half(c + kind * GROUP, s), :]
        return hop(1, c, s, kind, True, held, land.at[half(chunk(c), s), :], to)

    def leg2(c, s, kind):
        to = place(x - kind, wrap(z - (4 + kind * (back_far - 4)) * (1 - 2 * s)))
        held = relay_b.at[half(c + kind * GROUP, s), :]
        return hop(2, c, s, kind, False, ret_s.at[half(c, s), :], held, to)

    def leg3(c, s, kind):
        sign = 1 - 2 * s
        to = place(x, wrap(z - (out_far if kind else 4) * sign))
        held = relay_b.at[half(c + kind * GROUP, s), :]
        return hop(3, c, s, kind, True, held, ret_l.at[half(c, s), :], to)

    def relays_out(s, kind):
        sign = 1 - 2 * s
        if kind:
            return (x > 0) & (wrap(z - (2 * n_x - 2 * x) * sign) >= 8)
        return wrap(z - 4 * sign) < 8

    def relays_back(s, kind):
        sign = 1 - 2 * s
        if kind:
            return (x < n_x - 1) & (wrap(z + (2 * x + 2) * sign) < 8)
        return wrap(z + 4 * sign) >= 8

    def start_out(c):
        @pl.when(has_next)
        def _():
            for s in (0, 1):
                leg0(c, s, out_kind).start()

    def start_back(c):
        @pl.when(has_previous)
        def _():
            for s in (0, 1):
                leg2(c, s, back_kind).start()

    def pass_on(relays, first, second, c):
        for s in (0, 1):
            for kind in (0, 1):

                @pl.when(relays(s, kind))
                def _():
                    first(c, s, kind).wait_recv()
                    second(c, s, kind).start()

    for c in range(GROUP):
        for kind in (0, 1):
            if c == 0:
                keep(kind).wait()
            else:
                into(kind, c).wait_recv()
        start_out(c)

    for kind in (2, 3):
        keep(kind).start()
    for k in range(1, GROUP):
        for kind in (2, 3):
            into(kind, k).start()

    gains = gain_in[...]
    for k in range(1, 8):
        share(k).wait_recv()
        gains = gains + gain_s[k]
    q_gain, k_gain = gains[0:1, :], gains[1:2, :]

    def hat(at):
        raw = land[at, :HEAD].astype(F32)
        key = prepare(raw, k_gain, cos_s[at, :], sin_s[at, :])
        k_s[at, :] = key.astype(BF16)
        kt_s[:, at] = key.T.astype(BF16)

    cos_t, sin_t = cos_in[16:, :], sin_in[16:, :]

    def table(at, i):
        cos_b, sin_b = cos_in[pl.ds(i, 1), :], sin_in[pl.ds(i, 1), :]
        cos_s[at, :] = cos_b * cos_t - sin_b * sin_t
        sin_s[at, :] = sin_b * cos_t + cos_b * sin_t
        dk_s[at, :] = jnp.zeros((TOK, HEAD), F32)
        dv_s[at, :] = jnp.zeros((TOK, HEAD), F32)

    def first_half(c, _):
        pass_on(relays_out, leg0, leg1, c)
        table(block(c), c)
        table(block(c, SPAN), c + GROUP)
        hat(block(c, SPAN))
        return 0

    lax.fori_loop(0, GROUP, first_half, 0)

    for kind in (2, 3):
        keep(kind).wait()
        for k in range(1, GROUP):
            into(kind, k).wait_recv()

    def previous_keys(c, _):

        @pl.when(has_previous)
        def _():
            for s in (0, 1):
                leg1(c, s, 0).wait_recv()

        @pl.when(g == 0)
        def _():
            land[block(chunk(c)), :] = jnp.zeros((TOK, 2 * HEAD), BF16)

        hat(block(chunk(c)))
        return 0

    lax.fori_loop(0, GROUP, previous_keys, 0)

    outs = ((qg_s, 0, 2 * HEAD, lq), (kvg_s, 0, HEAD, lk), (kvg_s, HEAD, HEAD, lv))

    def send_out(kind, p):
        src, at, width, dst = outs[kind]
        return remote(
            src.at[block(p), at : at + width], dst.at[:, lanes(r, width)],
            out_send.at[kind, p], out_recv.at[kind, r], mate(p),
        )

    def keep_out(kind):
        src, at, width, dst = outs[kind]
        return pltpu.make_async_copy(
            src.at[block(r), at : at + width], dst.at[:, lanes(r, width)], self_sem.at[4 + kind]
        )

    def arrive_out(kind, p):
        src, at, width, dst = outs[kind]
        return remote(
            src.at[block(p), at : at + width], dst.at[:, lanes(p, width)],
            out_send.at[kind, p], out_recv.at[kind, p], mate(p),
        )

    def deliver(kind, p):
        @pl.when(p != r)
        def _():
            send_out(kind, p).start()

        @pl.when(p == r)
        def _():
            keep_out(kind).start()

    wide = WINDOW + TOK

    def step(b, _):
        rows, keys = block(b), pl.ds(pl.multiple_of(b * TOK, TOK), wide)
        cosine, sine = cos_s[block(b, SPAN), :], sin_s[block(b, SPAN), :]
        raw = [qd[rows, h * HEAD : (h + 1) * HEAD].astype(F32) for h in range(2)]
        q = jnp.concatenate([prepare(v, q_gain, cosine, sine) for v in raw], axis=0).astype(BF16)
        do = jnp.concatenate([qd[rows, (2 + h) * HEAD : (3 + h) * HEAD] for h in range(2)], axis=0)
        s = mm(k_s[keys, :], q, NT)
        row = lax.broadcasted_iota(jnp.int32, (wide, 2 * TOK), 0)
        col = lax.broadcasted_iota(jnp.int32, (wide, 2 * TOK), 1) % TOK
        seen = (row > col) & (row <= col + WINDOW) & (row >= low - b * TOK)
        s = jnp.where(seen, s * (SCALE * LOG2E), -1e30)
        w = jnp.exp2(s - jnp.max(s, axis=0, keepdims=True))
        probs = w * (1.0 / jnp.sum(w, axis=0, keepdims=True))
        pb = probs.astype(BF16)
        dp = mm(land[keys, HEAD:], do, NT)
        delta = jnp.sum(pb.astype(F32) * dp, axis=0, keepdims=True)
        ds = (probs * (dp - delta)).astype(BF16)
        dv_s[keys, :] += mm(pb, do, NN)
        dk_s[keys, :] += mm(ds, q, NN)
        ret_s[rows, :HEAD] = (dk_s[rows, :] * SCALE).astype(BF16)
        ret_s[rows, HEAD:] = dv_s[rows, :].astype(BF16)
        start_back(b)
        dq = (mm(kt_s[:, keys], ds, NN) * SCALE).T
        for h in range(2):
            back = prepare_back(raw[h], q_gain, cosine, sine, dq[h * TOK : (h + 1) * TOK, :])
            qg_s[rows, h * HEAD : (h + 1) * HEAD] = back.astype(BF16)

        @pl.when(b >= 2)
        def _():
            pass_on(relays_back, leg2, leg3, b - 2)

        deliver(0, b)
        return 0

    lax.fori_loop(0, GROUP, step, 0)
    for c in (GROUP - 2, GROUP - 1):
        pass_on(relays_back, leg2, leg3, c)

    def finish(b, _):
        rows, at = block(b), block(b, SPAN)

        @pl.when(has_next)
        def _():
            for s in (0, 1):
                leg3(b, s, 0).wait_recv()

        @pl.when(jnp.logical_not(has_next))
        def _():
            ret_l[rows, :] = jnp.zeros((TOK, 2 * HEAD), BF16)

        dk = dk_s[at, :] * SCALE + ret_l[rows, :HEAD].astype(F32)
        back = prepare_back(land[at, :HEAD].astype(F32), k_gain, cos_s[at, :], sin_s[at, :], dk)
        kvg_s[rows, :HEAD] = back.astype(BF16)
        kvg_s[rows, HEAD:] = (dv_s[at, :] + ret_l[rows, HEAD:].astype(F32)).astype(BF16)
        deliver(1, b)
        deliver(2, b)
        return 0

    lax.fori_loop(0, GROUP, finish, 0)

    for k in range(1, GROUP):
        for kind in range(4):
            into(kind, k).wait_send()
        share(k).wait_send()
    for c in range(GROUP):
        for s in (0, 1):

            @pl.when(has_next)
            def _():
                leg0(c, s, out_kind).wait_send()

            @pl.when(has_previous)
            def _():
                leg2(c, s, back_kind).wait_send()

            for kind in (0, 1):

                @pl.when(relays_out(s, kind))
                def _():
                    leg1(c, s, kind).wait_send()

                @pl.when(relays_back(s, kind))
                def _():
                    leg3(c, s, kind).wait_send()

    for kind, result in ((0, oq), (1, ok), (2, ov)):
        for k in range(1, GROUP):
            p = lax.rem(r + k, GROUP)
            arrive_out(kind, p).wait_recv()
            send_out(kind, p).wait_send()
        keep_out(kind).wait()
        result[0] = outs[kind][3][...]


def settle_kernel(a, b, c, oa, ob, oc, sem):
    copies = [pltpu.make_async_copy(i, o, sem.at[n]) for n, (i, o) in enumerate(((a, oa), (b, ob), (c, oc)))]
    for copy in copies:
        copy.start()
    for copy in copies:
        copy.wait()


def body(queries, raw_key_rows, values, out_grad, query_gain, key_norm_gain):
    dp = lax.axis_index("dp")
    part = jnp.stack([query_gain, key_norm_gain])
    gains = lax.dynamic_update_slice(jnp.zeros((8, HEAD), F32), part, (0, dp * part.shape[1]))
    group = lax.axis_index("seq") // GROUP
    index = jnp.arange(16 + TOK, dtype=jnp.int32)
    positions = jnp.where(index < 16, (group - 1) * SPAN + index * TOK, index - 16).astype(F32)
    half = np.arange(HEAD) % (HEAD // 2)
    frequency = jnp.asarray((ROPE_BASE ** (-half * (2.0 / HEAD))).astype(np.float32))
    sign = jnp.asarray(np.where(np.arange(HEAD) < HEAD // 2, -1.0, 1.0).astype(np.float32))
    angles = positions[:, None] * frequency[None, :]
    anywhere = pl.BlockSpec(memory_space=pl.ANY)
    vmem = pl.BlockSpec(memory_space=pltpu.VMEM)
    dma = pltpu.SemaphoreType.DMA
    shapes = tuple(jax.ShapeDtypeStruct(a.shape, BF16) for a in (queries, raw_key_rows, values))
    grads = pl.pallas_call(
        layer_kernel,
        out_shape=shapes,
        in_specs=[anywhere] * 4 + [vmem] * 3,
        out_specs=(vmem, vmem, vmem),
        scratch_shapes=[
            pltpu.VMEM((2 * SPAN, 2 * HEAD), BF16),
            pltpu.VMEM((SPAN, 4 * HEAD), BF16),
            pltpu.VMEM((8, 8, HEAD), F32),
            pltpu.VMEM((2 * SPAN, HEAD), F32),
            pltpu.VMEM((2 * SPAN, HEAD), F32),
            pltpu.VMEM((2 * SPAN, HEAD), BF16),
            pltpu.VMEM((HEAD, 2 * SPAN), BF16),
            pltpu.VMEM((2 * SPAN, HEAD), F32),
            pltpu.VMEM((2 * SPAN, HEAD), F32),
            pltpu.VMEM((2 * SPAN, 2 * HEAD), BF16),
            pltpu.VMEM((2 * SPAN, 2 * HEAD), BF16),
            pltpu.VMEM((SPAN, 2 * HEAD), BF16),
            pltpu.VMEM((SPAN, 2 * HEAD), BF16),
            pltpu.VMEM((SPAN, 2 * HEAD), BF16),
            pltpu.VMEM((SPAN, 2 * HEAD), BF16),
            pltpu.VMEM((TOK, 2 * SPAN), BF16),
            pltpu.VMEM((TOK, SPAN), BF16),
            pltpu.VMEM((TOK, SPAN), BF16),
            dma((4, 8)), dma((4, 8)), dma((8,)), dma((8,)),
            dma((4, 2, 16)), dma((4, 2, 16)), dma((3, 8)), dma((3, 8)), dma((7,)),
        ],
        compiler_params=pltpu.CompilerParams(collective_id=0, has_side_effects=True),
        name="layer_backward",
    )(
        queries, raw_key_rows, values, out_grad, gains,
        jnp.cos(angles), jnp.sin(angles) * sign[None, :],
    )
    return pl.pallas_call(
        settle_kernel,
        out_shape=shapes,
        in_specs=[vmem] * 3,
        out_specs=(anywhere,) * 3,
        scratch_shapes=[dma((3,))],
        name="settle",
    )(*grads)


def solution(mesh):
    spec = P("dp", "seq", None)
    return jax.shard_map(
        body,
        mesh=mesh,
        in_specs=(spec, spec, spec, spec, P("dp"), P("dp")),
        out_specs=(spec, spec, spec),
        check_vma=False,
    )
```

```python
import functools

import jax
import jax.numpy as jnp
import numpy as np
from jax import lax
from jax.experimental import pallas as pl
from jax.experimental.pallas import tpu as pltpu
from jax.sharding import PartitionSpec as P

HEAD = 128
GROUP = 8
TOK = 128
SPAN = GROUP * TOK
WINDOW = 1024
SCALE = 168.0 ** (-0.5)
LOG2E = 1.4426950408889634
ROPE_BASE = 10000.0
EPSILON = 1e-06
NT = (((1,), (1,)), ((), ()))
NN = (((1,), (0,)), ((), ()))
MESH = pl.DeviceIdType.MESH
BF16 = jnp.bfloat16
F32 = jnp.float32


def mm(a, b, dims):
    return lax.dot_general(a, b, dims, preferred_element_type=F32)


def inverse_norm(x):
    return lax.rsqrt(jnp.mean(x * x, axis=-1, keepdims=True) + EPSILON)


def prepare(x, gain, cosine, sine):
    n = x * inverse_norm(x) * gain
    return n * cosine + pltpu.roll(n, HEAD // 2, 1) * sine


def prepare_back(x, gain, cosine, sine, dy):
    inv = inverse_norm(x)
    h = (dy * cosine + pltpu.roll(dy * sine, HEAD // 2, 1)) * gain
    return inv * h - x * (inv * inv * inv * jnp.mean(x * h, axis=-1, keepdims=True))


def block(i, base=0):
    return pl.ds(pl.multiple_of(base + i * TOK, TOK), TOK)


def half(i, s, base=0):
    return pl.ds(pl.multiple_of(base + i * TOK + s * (TOK // 2), TOK // 2), TOK // 2)


def lanes(i, width):
    return pl.ds(pl.multiple_of(i * width, width), width)


def layer_kernel(
    q_in, k_in, v_in, do_in, gain_in, cos_in, sin_in,
    oq, ok, ov,
    land, qd, gain_s, cos_s, sin_s, k_s, kt_s, dk_s, dv_s,
    ret_s, ret_l, qg_s, kvg_s, lq, lk, lv,
    in_send, in_recv, gain_send, gain_recv, z_send, z_recv, out_send, out_recv, self_sem,
):
    d = lax.axis_index("dp")
    seq = lax.axis_index("seq")
    r = lax.rem(seq, GROUP)
    g = lax.div(seq, GROUP)
    n_g = lax.div(lax.axis_size("seq"), GROUP)
    n_x = n_g // 2
    x = lax.div(g, 2)
    z = lax.rem(g, 2) * 8 + d
    low = jnp.where(g == 0, SPAN, 0)

    def mate(p):
        return (d, g * GROUP + p)

    def remote(src, dst, send, recv, device):
        return pltpu.make_async_remote_copy(
            src_ref=src, dst_ref=dst, send_sem=send, recv_sem=recv, device_id=device, device_id_type=MESH
        )

    barrier = pltpu.get_barrier_semaphore()

    def greet(device):
        pl.semaphore_signal(barrier, inc=1, device_id=device, device_id_type=MESH)

    for k in range(1, GROUP):
        greet(mate(lax.rem(r + k, GROUP)))
    for k in range(1, 8):
        greet((lax.rem(d + k, 8), seq))
    after = (d, lax.rem(g + 1, n_g) * GROUP + r)
    before = (d, lax.rem(g + n_g - 1, n_g) * GROUP + r)
    greet(after)
    greet(before)
    pl.semaphore_wait(barrier, 16)

    kinds = (
        (k_in, HEAD, land, SPAN, 0),
        (v_in, HEAD, land, SPAN, HEAD),
        (q_in, 2 * HEAD, qd, 0, 0),
        (do_in, 2 * HEAD, qd, 0, 2 * HEAD),
    )

    def into(kind, k):
        src, width, dst, base, at = kinds[kind]
        p = lax.rem(r + k, GROUP)
        return remote(
            src.at[0, :, lanes(p, width)], dst.at[block(r, base), at : at + width],
            in_send.at[kind, k], in_recv.at[kind, k], mate(p),
        )

    def keep(kind):
        src, width, dst, base, at = kinds[kind]
        return pltpu.make_async_copy(
            src.at[0, :, lanes(r, width)], dst.at[block(r, base), at : at + width], self_sem.at[kind]
        )

    def share(k):
        return remote(
            gain_in, gain_s.at[k], gain_send.at[k], gain_recv.at[k], (lax.rem(d + k, 8), seq)
        )

    for kind in (0, 1):
        keep(kind).start()
    for k in range(1, GROUP):
        for kind in (0, 1):
            into(kind, k).start()
    for k in range(1, 8):
        share(k).start()
    def chunk(c):
        return lax.rem(r - c + GROUP, GROUP)

    def hop(leg, c, s, src, dst, device):
        return remote(src, dst, z_send.at[leg, s, c], z_recv.at[leg, s, c], device)

    def leg0(c, s):
        return hop(0, c, s, land.at[half(chunk(c), s, SPAN), :], land.at[half(chunk(c), s), :], after)

    def leg1(c, s):
        return hop(1, c, s, ret_s.at[half(c, s), :], ret_l.at[half(c, s), :], before)

    def start(leg, c):
        for s in (0, 1):
            leg(c, s).start()

    def arrive(leg, c):
        for s in (0, 1):
            leg(c, s).wait_recv()

    for c in range(GROUP):
        for kind in (0, 1):
            if c == 0:
                keep(kind).wait()
            else:
                into(kind, c).wait_recv()
        start(leg0, c)

    for kind in (2, 3):
        keep(kind).start()
    for k in range(1, GROUP):
        for kind in (2, 3):
            into(kind, k).start()

    gains = gain_in[...]
    for k in range(1, 8):
        share(k).wait_recv()
        gains = gains + gain_s[k]
    q_gain, k_gain = gains[0:1, :], gains[1:2, :]

    def hat(at):
        raw = land[at, :HEAD].astype(F32)
        key = prepare(raw, k_gain, cos_s[at, :], sin_s[at, :])
        k_s[at, :] = key.astype(BF16)
        kt_s[:, at] = key.T.astype(BF16)

    cos_t, sin_t = cos_in[16:, :], sin_in[16:, :]

    def table(at, i):
        cos_b, sin_b = cos_in[pl.ds(i, 1), :], sin_in[pl.ds(i, 1), :]
        cos_s[at, :] = cos_b * cos_t - sin_b * sin_t
        sin_s[at, :] = sin_b * cos_t + cos_b * sin_t
        dk_s[at, :] = jnp.zeros((TOK, HEAD), F32)
        dv_s[at, :] = jnp.zeros((TOK, HEAD), F32)

    def first_half(c, _):
        table(block(c), c)
        table(block(c, SPAN), c + GROUP)
        hat(block(c, SPAN))
        return 0

    lax.fori_loop(0, GROUP, first_half, 0)

    for kind in (2, 3):
        keep(kind).wait()
        for k in range(1, GROUP):
            into(kind, k).wait_recv()

    def previous_keys(c, _):
        arrive(leg0, c)
        hat(block(chunk(c)))
        return 0

    lax.fori_loop(0, GROUP, previous_keys, 0)

    outs = ((qg_s, 0, 2 * HEAD, lq), (kvg_s, 0, HEAD, lk), (kvg_s, HEAD, HEAD, lv))

    def send_out(kind, p):
        src, at, width, dst = outs[kind]
        return remote(
            src.at[block(p), at : at + width], dst.at[:, lanes(r, width)],
            out_send.at[kind, p], out_recv.at[kind, r], mate(p),
        )

    def keep_out(kind):
        src, at, width, dst = outs[kind]
        return pltpu.make_async_copy(
            src.at[block(r), at : at + width], dst.at[:, lanes(r, width)], self_sem.at[4 + kind]
        )

    def arrive_out(kind, p):
        src, at, width, dst = outs[kind]
        return remote(
            src.at[block(p), at : at + width], dst.at[:, lanes(p, width)],
            out_send.at[kind, p], out_recv.at[kind, p], mate(p),
        )

    def deliver(kind, p):
        @pl.when(p != r)
        def _():
            send_out(kind, p).start()

        @pl.when(p == r)
        def _():
            keep_out(kind).start()

    wide = WINDOW + TOK

    def step(b, _):
        rows, keys = block(b), pl.ds(pl.multiple_of(b * TOK, TOK), wide)
        cosine, sine = cos_s[block(b, SPAN), :], sin_s[block(b, SPAN), :]
        raw = [qd[rows, h * HEAD : (h + 1) * HEAD].astype(F32) for h in range(2)]
        q = jnp.concatenate([prepare(v, q_gain, cosine, sine) for v in raw], axis=0).astype(BF16)
        do = jnp.concatenate([qd[rows, (2 + h) * HEAD : (3 + h) * HEAD] for h in range(2)], axis=0)
        s = mm(k_s[keys, :], q, NT)
        row = lax.broadcasted_iota(jnp.int32, (wide, 2 * TOK), 0)
        col = lax.broadcasted_iota(jnp.int32, (wide, 2 * TOK), 1) % TOK
        seen = (row > col) & (row <= col + WINDOW) & (row >= low - b * TOK)
        s = jnp.where(seen, s * (SCALE * LOG2E), -1e30)
        w = jnp.exp2(s - jnp.max(s, axis=0, keepdims=True))
        probs = w * (1.0 / jnp.sum(w, axis=0, keepdims=True))
        pb = probs.astype(BF16)
        dp = mm(land[keys, HEAD:], do, NT)
        delta = jnp.sum(pb.astype(F32) * dp, axis=0, keepdims=True)
        ds = (probs * (dp - delta)).astype(BF16)
        dv_s[keys, :] += mm(pb, do, NN)
        dk_s[keys, :] += mm(ds, q, NN)
        ret_s[rows, :HEAD] = (dk_s[rows, :] * SCALE).astype(BF16)
        ret_s[rows, HEAD:] = dv_s[rows, :].astype(BF16)
        start(leg1, b)
        dq = (mm(kt_s[:, keys], ds, NN) * SCALE).T
        for h in range(2):
            back = prepare_back(raw[h], q_gain, cosine, sine, dq[h * TOK : (h + 1) * TOK, :])
            qg_s[rows, h * HEAD : (h + 1) * HEAD] = back.astype(BF16)

        deliver(0, b)
        return 0

    lax.fori_loop(0, GROUP, step, 0)

    def finish(b, _):
        rows, at = block(b), block(b, SPAN)
        arrive(leg1, b)
        dk = dk_s[at, :] * SCALE + ret_l[rows, :HEAD].astype(F32)
        back = prepare_back(land[at, :HEAD].astype(F32), k_gain, cos_s[at, :], sin_s[at, :], dk)
        kvg_s[rows, :HEAD] = back.astype(BF16)
        kvg_s[rows, HEAD:] = (dv_s[at, :] + ret_l[rows, HEAD:].astype(F32)).astype(BF16)
        deliver(1, b)
        deliver(2, b)
        return 0

    lax.fori_loop(0, GROUP, finish, 0)

    for k in range(1, GROUP):
        for kind in range(4):
            into(kind, k).wait_send()
        share(k).wait_send()
    for c in range(GROUP):
        for leg in (leg0, leg1):
            for s in (0, 1):
                leg(c, s).wait_send()
    for kind, result in ((0, oq), (1, ok), (2, ov)):
        for k in range(1, GROUP):
            p = lax.rem(r + k, GROUP)
            arrive_out(kind, p).wait_recv()
            send_out(kind, p).wait_send()
        keep_out(kind).wait()
        result[0] = outs[kind][3][...]


def settle_kernel(a, b, c, oa, ob, oc, sem):
    copies = [pltpu.make_async_copy(i, o, sem.at[n]) for n, (i, o) in enumerate(((a, oa), (b, ob), (c, oc)))]
    for copy in copies:
        copy.start()
    for copy in copies:
        copy.wait()


def body(queries, raw_key_rows, values, out_grad, query_gain, key_norm_gain):
    dp = lax.axis_index("dp")
    part = jnp.stack([query_gain, key_norm_gain])
    gains = lax.dynamic_update_slice(jnp.zeros((8, HEAD), F32), part, (0, dp * part.shape[1]))
    group = lax.axis_index("seq") // GROUP
    index = jnp.arange(16 + TOK, dtype=jnp.int32)
    positions = jnp.where(index < 16, (group - 1) * SPAN + index * TOK, index - 16).astype(F32)
    half = np.arange(HEAD) % (HEAD // 2)
    frequency = jnp.asarray((ROPE_BASE ** (-half * (2.0 / HEAD))).astype(np.float32))
    sign = jnp.asarray(np.where(np.arange(HEAD) < HEAD // 2, -1.0, 1.0).astype(np.float32))
    angles = positions[:, None] * frequency[None, :]
    anywhere = pl.BlockSpec(memory_space=pl.ANY)
    vmem = pl.BlockSpec(memory_space=pltpu.VMEM)
    dma = pltpu.SemaphoreType.DMA
    shapes = tuple(jax.ShapeDtypeStruct(a.shape, BF16) for a in (queries, raw_key_rows, values))
    grads = pl.pallas_call(
        layer_kernel,
        out_shape=shapes,
        in_specs=[anywhere] * 4 + [vmem] * 3,
        out_specs=(vmem, vmem, vmem),
        scratch_shapes=[
            pltpu.VMEM((2 * SPAN, 2 * HEAD), BF16),
            pltpu.VMEM((SPAN, 4 * HEAD), BF16),
            pltpu.VMEM((8, 8, HEAD), F32),
            pltpu.VMEM((2 * SPAN, HEAD), F32),
            pltpu.VMEM((2 * SPAN, HEAD), F32),
            pltpu.VMEM((2 * SPAN, HEAD), BF16),
            pltpu.VMEM((HEAD, 2 * SPAN), BF16),
            pltpu.VMEM((2 * SPAN, HEAD), F32),
            pltpu.VMEM((2 * SPAN, HEAD), F32),
            pltpu.VMEM((SPAN, 2 * HEAD), BF16),
            pltpu.VMEM((SPAN, 2 * HEAD), BF16),
            pltpu.VMEM((SPAN, 2 * HEAD), BF16),
            pltpu.VMEM((SPAN, 2 * HEAD), BF16),
            pltpu.VMEM((TOK, 2 * SPAN), BF16),
            pltpu.VMEM((TOK, SPAN), BF16),
            pltpu.VMEM((TOK, SPAN), BF16),
            dma((4, 8)), dma((4, 8)), dma((8,)), dma((8,)),
            dma((2, 2, 8)), dma((2, 2, 8)), dma((3, 8)), dma((3, 8)), dma((7,)),
        ],
        compiler_params=pltpu.CompilerParams(collective_id=0, has_side_effects=True),
        name="layer_backward",
    )(
        queries, raw_key_rows, values, out_grad, gains,
        jnp.cos(angles), jnp.sin(angles) * sign[None, :],
    )
    return pl.pallas_call(
        settle_kernel,
        out_shape=shapes,
        in_specs=[vmem] * 3,
        out_specs=(anywhere,) * 3,
        scratch_shapes=[dma((3,))],
        name="settle",
    )(*grads)


def solution(mesh):
    spec = P("dp", "seq", None)
    return jax.shard_map(
        body,
        mesh=mesh,
        in_specs=(spec, spec, spec, spec, P("dp"), P("dp")),
        out_specs=(spec, spec, spec),
        check_vma=False,
    )
```
